32 devices in a mesh: ctx: 8 (over y, x, core), wsh: 4 (over z).
Axes of the slice: x: 2, y: 2, z: 4, core: 2. Of those that a mesh axis runs over, the one named last changes fastest.
Arguments:
- layer_input: bfloat16 [4, 1024, 960], P('wsh', 'ctx'), may hold values from -50 to 50
- positions: int32 [1024], replicated, may hold values from 0 to 1023, as said below
- first_gain: bfloat16 [960], P('wsh'), may hold values from 0.5 to 2
- query_weight: bfloat16 [960, 960], P('wsh'), may hold values from -1 to 1
- key_weight: bfloat16 [960, 320], P('wsh'), may hold values from -1 to 1
- value_proj_weight: bfloat16 [960, 320], P('wsh'), may hold values from -0.1875 to 0.1875
- output_weight: bfloat16 [960, 960], P('wsh'), may hold values from -1.5 to 1.5
- second_gain: bfloat16 [960], P('wsh'), may hold values from 0.5 to 2
- gate_weight: bfloat16 [960, 2560], P('wsh'), may hold values from -0.1875 to 0.1875
- up_weight: bfloat16 [960, 2560], P('wsh'), may hold values from -0.1875 to 0.1875
- down_weight: bfloat16 [2560, 960], P('wsh'), may hold values from -0.125 to 0.125
- cotangent: bfloat16 [4, 1024, 960], P('wsh', 'ctx'), may hold values from -6 to 6
Outputs:
- layer_output: bfloat16 [4, 1024, 960], P('wsh', 'ctx')
- input_gradient: float32 [4, 1024, 960], P('wsh', 'ctx')
- first_gain_gradient: float32 [960], P('wsh')
- query_weight_gradient: float32 [960, 960], P('wsh')
- key_weight_gradient: float32 [960, 320], P('wsh')
- value_weight_gradient: float32 [960, 320], P('wsh')
- output_weight_gradient: float32 [960, 960], P('wsh')
- second_gain_gradient: float32 [960], P('wsh')
- gate_weight_gradient: float32 [960, 2560], P('wsh')
- up_weight_gradient: float32 [960, 2560], P('wsh')
- down_weight_gradient: float32 [2560, 960], P('wsh')
The draws below stay inside these ranges and needn't reach their ends.
Inputs may be any that keep to these rules, and one draw needn't show every extreme that they name: Along ctx, device c holds two blocks of 64 consecutive positions, each starting at a multiple of 64: first block b_c, then block 15 - b_c; the b_c run over 0 to 7, each once.
All inputs are finite; a program needn't handle non-finite values.
Results may differ from the reference program's by a relative error of at most 0.023.
The reference program's roundings to bfloat16 on the way count: a program that leaves them out, or rounds other values in their place, can miss the bound.
Values may be sent and summed in bfloat16 or wider, within the bound.
A program may use at most 192 MiB of HBM per device.

```python
import math
import jax
import jax.numpy as jnp
from jax import lax

MODEL_WIDTH = 960
QUERY_HEADS = 15
KEY_VALUE_HEADS = 5
HEAD_SIZE = 64
FEEDFWD_UNITS = 2560
TOK_DEV = 128
BLK = 64
SEQ = 1024
SEQS = 4
N_CTX = 8


def column_scales(key):
    return jnp.exp(jax.random.uniform(jax.random.fold_in(key, 7001), (MODEL_WIDTH,), jnp.float32, math.log(0.3), math.log(3.0)))


def position_table(key):
    order = jax.random.permutation(jax.random.fold_in(key, 7003), N_CTX).astype(jnp.int32)
    steps = jnp.arange(BLK, dtype=jnp.int32)
    lower = order[:, None] * BLK + steps[None, :]
    upper = (2 * N_CTX - 1 - order)[:, None] * BLK + steps[None, :]
    return jnp.concatenate([lower, upper], axis=1).reshape(SEQ)


def drawn_weight(key, salt, columns):
    return jax.random.truncated_normal(jax.random.fold_in(key, salt), -5.0, 5.0, (MODEL_WIDTH, columns), jnp.float32) / math.sqrt(MODEL_WIDTH)


def draw_positions(key, part):
    return position_table(key)


def draw_layer_input(key, part):
    columns = column_scales(key)
    token_rows = jnp.exp(jax.random.uniform(jax.random.fold_in(key, 7004), (SEQS, SEQ, 1), jnp.float32, math.log(0.3), math.log(3.0)))
    noise_key = jax.random.fold_in(key, 7005)
    noise = jax.random.truncated_normal(noise_key, -5.0, 5.0, (SEQS, SEQ, MODEL_WIDTH), jnp.float32)
    result = noise * token_rows * columns
    return jnp.clip(result, -50.0, 50.0).astype(jnp.bfloat16)


def draw_query_weight(key, part):
    weight_matrix = drawn_weight(key, 7010, QUERY_HEADS * HEAD_SIZE)
    return jnp.clip(weight_matrix, -1.0, 1.0).astype(jnp.bfloat16)


def draw_key_weight(key, part):
    weight_matrix = drawn_weight(key, 7011, KEY_VALUE_HEADS * HEAD_SIZE)
    return jnp.clip(weight_matrix, -1.0, 1.0).astype(jnp.bfloat16)


def levels(key, dims, pieces, least, high):
    loudness, own = 1.0, jax.random.fold_in(key, 6)
    for position, blocks in pieces:
        draws = jnp.exp(jax.random.uniform(jax.random.fold_in(own, position), (blocks,), jnp.float32, least / len(pieces), high / len(pieces)))
        loudness = loudness * jnp.repeat(draws, dims[position] // blocks).reshape([-1 if axis == position else 1 for axis in range(len(dims))])
    return loudness


def scatter_about(stream_key, extent, scale, limit, cuts=(), kind=jnp.bfloat16):
    values = scale * jax.random.normal(stream_key, extent, jnp.float32)
    if cuts:
        values = values * levels(stream_key, extent, cuts, -0.22, 0.18)
    return jnp.clip(values, -limit, limit).astype(kind)


def setup_inputs(seed: int = 0) -> dict:
    arg_keys = jax.random.split(jax.random.key(seed), 13)
    layer_input = draw_layer_input(jax.random.fold_in(arg_keys[12], 71), 0)
    positions = draw_positions(jax.random.fold_in(arg_keys[12], 71), 0)
    first_gain = jnp.clip(jnp.exp(math.log(2.0) - 1.3862944 * jax.random.uniform(arg_keys[2], (MODEL_WIDTH,), jnp.float32) ** levels(arg_keys[2], (MODEL_WIDTH,), ((0, 4),), -0.2, 0.2)), 0.5, 2.0).astype(jnp.bfloat16)
    query_weight = draw_query_weight(jax.random.fold_in(arg_keys[12], 71), 0)
    key_weight = draw_key_weight(jax.random.fold_in(arg_keys[12], 71), 0)
    value_proj_weight = scatter_about(arg_keys[5], (MODEL_WIDTH, KEY_VALUE_HEADS * HEAD_SIZE), MODEL_WIDTH ** -0.5, 0.1875, ((0, 4),))
    output_weight = scatter_about(arg_keys[6], (QUERY_HEADS * HEAD_SIZE, MODEL_WIDTH), (max(QUERY_HEADS * HEAD_SIZE // 64, 1)) ** -0.5, 1.5, ((0, 4),))
    second_gain = jnp.clip(jnp.exp(math.log(2.0) - 1.3862944 * jax.random.uniform(arg_keys[7], (MODEL_WIDTH,), jnp.float32) ** levels(arg_keys[7], (MODEL_WIDTH,), ((0, 4),), -0.2, 0.2)), 0.5, 2.0).astype(jnp.bfloat16)
    gate_weight = scatter_about(arg_keys[8], (MODEL_WIDTH, FEEDFWD_UNITS), MODEL_WIDTH ** -0.5, 0.1875, ((0, 4),))
    up_weight = scatter_about(arg_keys[9], (MODEL_WIDTH, FEEDFWD_UNITS), MODEL_WIDTH ** -0.5, 0.1875, ((0, 4),))
    down_weight = scatter_about(arg_keys[10], (FEEDFWD_UNITS, MODEL_WIDTH), FEEDFWD_UNITS ** -0.5, 0.125, ((0, 4),))
    cotangent = scatter_about(arg_keys[11], (SEQS, SEQ, MODEL_WIDTH), 1, 6.0, ((0, 4), (1, 8)))
    return {"layer_input": layer_input, "positions": positions, "first_gain": first_gain, "query_weight": query_weight, "key_weight": key_weight, "value_proj_weight": value_proj_weight, "output_weight": output_weight, "second_gain": second_gain, "gate_weight": gate_weight, "up_weight": up_weight, "down_weight": down_weight, "cotangent": cotangent}


EPS = 1e-05
ROPE_BASE = 10000.0
NEG_FILL = -1e+30

def finalize_block(array):
    return lax.optimization_barrier(array.astype(jnp.bfloat16))

def widened(array):
    return array.astype(jnp.float32)

def matrix_product(left, right):
    return jnp.dot(left, right, preferred_element_type=jnp.float32)

def times_transposed(left, right):
    return lax.dot_general(left, right, (((1,), (1,)), ((), ())), preferred_element_type=jnp.float32)

def token_sum(left, right):
    return lax.dot_general(left, right, (((0,), (0,)), ((), ())), preferred_element_type=jnp.float32)

def norm_scale(inputs):
    return lax.rsqrt(lax.optimization_barrier(jnp.mean(inputs * inputs, axis=-1, keepdims=True)) + EPS)

def norm_back(incoming, normed, scale, gain):
    scaled = incoming * gain
    return scale * (scaled - normed * lax.optimization_barrier(jnp.mean(scaled * normed, axis=-1, keepdims=True)))

def rope_tables(places, head_width):
    half = head_width // 2
    frequency = ROPE_BASE ** (-2.0 * jnp.arange(half, dtype=jnp.float32) / head_width)
    angle = places.astype(jnp.float32)[:, None] * frequency[None, :]
    return (jnp.cos(angle)[:, None, :], jnp.sin(angle)[:, None, :])

def apply_rotary(inputs, cosine_table, sine_table):
    half = inputs.shape[-1] // 2
    first = inputs[..., :half]
    second = inputs[..., half:]
    return jnp.concatenate([first * cosine_table - second * sine_table, second * cosine_table + first * sine_table], axis=-1)

def apply_rotary_back(incoming, cosine_table, sine_table):
    half = incoming.shape[-1] // 2
    first = incoming[..., :half]
    second = incoming[..., half:]
    return jnp.concatenate([first * cosine_table + second * sine_table, second * cosine_table - first * sine_table], axis=-1)

def attend_forward(query_rows_local, query_places, keys_rotated_pos, value_rows_local, key_places, tiles, tile_piece, score_scale):
    query_rows, head_groups, repeats, head_width = query_rows_local.shape
    queries_wide = widened(query_rows_local)

    def visit(index, carry):
        running, totals, weighted = carry
        begin = index * tile_piece
        key_tile = widened(lax.dynamic_slice_in_dim(keys_rotated_pos, begin, tile_piece, 0))
        value_tile = widened(lax.dynamic_slice_in_dim(value_rows_local, begin, tile_piece, 0))
        place_tile = lax.dynamic_slice_in_dim(key_places, begin, tile_piece, 0)
        scores = jnp.einsum('qgrd,kgd->qgrk', queries_wide, key_tile) * score_scale
        allowed = (place_tile[None, :] <= query_places[:, None])[:, None, None, :]
        scores = jnp.where(allowed, scores, NEG_FILL)
        newest = jnp.maximum(running, lax.optimization_barrier(jnp.max(scores, axis=-1)))
        factor = jnp.exp(running - newest)
        portion = jnp.exp(scores - newest[..., None])
        totals = totals * factor + lax.optimization_barrier(jnp.sum(portion, axis=-1))
        weighted = weighted * factor[..., None] + jnp.einsum('qgrk,kgd->qgrd', widened(finalize_block(portion)), value_tile)
        return (newest, totals, weighted)
    start_state = (jnp.full((query_rows, head_groups, repeats), NEG_FILL, jnp.float32), jnp.zeros((query_rows, head_groups, repeats), jnp.float32), jnp.zeros((query_rows, head_groups, repeats, head_width), jnp.float32))
    running, totals, weighted = lax.fori_loop(0, tiles, visit, start_state)
    return (finalize_block(weighted / totals[..., None]), running + jnp.log(totals))

def attend_backward(query_rows_local, query_places, attention_result_back, log_total, delta_rows, keys_rotated_pos, value_rows_local, key_places, tiles, tile_piece, score_scale, keys_gradient_back, values_gradient_back):
    queries_wide = widened(query_rows_local)
    back_wide = widened(attention_result_back)

    def visit(index, carry):
        query_gradient_back, keys_gradient_back, values_gradient_back = carry
        begin = index * tile_piece
        key_tile = widened(lax.dynamic_slice_in_dim(keys_rotated_pos, begin, tile_piece, 0))
        value_tile = widened(lax.dynamic_slice_in_dim(value_rows_local, begin, tile_piece, 0))
        place_tile = lax.dynamic_slice_in_dim(key_places, begin, tile_piece, 0)
        scores = jnp.einsum('qgrd,kgd->qgrk', queries_wide, key_tile) * score_scale
        allowed = (place_tile[None, :] <= query_places[:, None])[:, None, None, :]
        scores = jnp.where(allowed, scores, NEG_FILL)
        probability = jnp.exp(scores - log_total[..., None])
        value_dots = jnp.einsum('qgrd,kgd->qgrk', back_wide, value_tile)
        score_grad = widened(finalize_block(probability * (value_dots - delta_rows[..., None]) * score_scale))
        query_gradient_back = query_gradient_back + jnp.einsum('qgrk,kgd->qgrd', score_grad, key_tile)
        key_part = jnp.einsum('qgrk,qgrd->kgd', score_grad, queries_wide)
        value_part = jnp.einsum('qgrk,qgrd->kgd', widened(finalize_block(probability)), back_wide)
        keys_gradient_back = lax.dynamic_update_slice_in_dim(keys_gradient_back, lax.dynamic_slice_in_dim(keys_gradient_back, begin, tile_piece, 0) + key_part, begin, 0)
        values_gradient_back = lax.dynamic_update_slice_in_dim(values_gradient_back, lax.dynamic_slice_in_dim(values_gradient_back, begin, tile_piece, 0) + value_part, begin, 0)
        return (query_gradient_back, keys_gradient_back, values_gradient_back)
    start_state = (jnp.zeros(query_rows_local.shape, jnp.float32), keys_gradient_back, values_gradient_back)
    return lax.fori_loop(0, tiles, visit, start_state)

def layer_sequence(tokens, incoming_rows, places, weights):
    first_scale, query_matrix, key_projection, value_projection, output_matrix, second_scale, gate_matrix, up_matrix, down_matrix = weights
    token_rows = tokens.shape[0]
    head_groups = QUERY_HEADS // KEY_VALUE_HEADS
    tile_piece = 2 * TOK_DEV
    block_tally_count = token_rows // tile_piece
    score_scale = 1.0 / math.sqrt(HEAD_SIZE)
    cosine_table, sine_table = rope_tables(places, HEAD_SIZE)
    inputs = widened(tokens)
    scale_one = norm_scale(inputs)
    normed_one = inputs * scale_one
    hidden_first = finalize_block(normed_one * widened(first_scale))
    query_rows_local = finalize_block(apply_rotary(matrix_product(hidden_first, query_matrix).reshape(token_rows, QUERY_HEADS, HEAD_SIZE), cosine_table, sine_table))
    keys_rotated_pos = finalize_block(apply_rotary(matrix_product(hidden_first, key_projection).reshape(token_rows, KEY_VALUE_HEADS, HEAD_SIZE), cosine_table, sine_table))
    value_rows_local = finalize_block(matrix_product(hidden_first, value_projection)).reshape(token_rows, KEY_VALUE_HEADS, HEAD_SIZE)
    query_block_list = query_rows_local.reshape(block_tally_count, tile_piece, KEY_VALUE_HEADS, head_groups, HEAD_SIZE)
    position_blocks = places.reshape(block_tally_count, tile_piece)
    index_list = jnp.arange(block_tally_count, dtype=jnp.int32)

    def forward_block(item):
        query_block, place_block, index = item
        return attend_forward(query_block, place_block, keys_rotated_pos, value_rows_local, places, index + 1, tile_piece, score_scale)
    attended_blocks, log_sum_blocks = lax.map(forward_block, (query_block_list, position_blocks, index_list))
    attention_result = attended_blocks.reshape(token_rows, QUERY_HEADS * HEAD_SIZE)
    mixed = inputs + matrix_product(attention_result, output_matrix)
    scale_two = norm_scale(mixed)
    normed_two = mixed * scale_two
    hidden_two = finalize_block(normed_two * widened(second_scale))
    gate = matrix_product(hidden_two, gate_matrix)
    upward = matrix_product(hidden_two, up_matrix)
    sigma = jax.nn.sigmoid(gate)
    activated = finalize_block(gate * sigma * upward)
    layer_output = (mixed + matrix_product(activated, down_matrix)).astype(jnp.bfloat16)
    down_gradient = token_sum(activated, incoming_rows)
    activated_back = times_transposed(incoming_rows, down_matrix)
    gate_back = finalize_block(activated_back * upward * sigma * (1.0 + gate * (1.0 - sigma)))
    up_back = finalize_block(activated_back * gate * sigma)
    gate_gradient = token_sum(hidden_two, gate_back)
    up_gradient = token_sum(hidden_two, up_back)
    second_back = times_transposed(gate_back, gate_matrix) + times_transposed(up_back, up_matrix)
    second_gradient = lax.optimization_barrier(jnp.sum(second_back * normed_two, axis=0))
    mixed_back = widened(incoming_rows) + norm_back(second_back, normed_two, scale_two, widened(second_scale))
    mixed_low = finalize_block(mixed_back)
    output_gradient = token_sum(attention_result, mixed_low)
    attention_result_back = finalize_block(times_transposed(mixed_low, output_matrix))
    delta_rows = lax.optimization_barrier(jnp.sum(widened(attention_result_back).reshape(token_rows, KEY_VALUE_HEADS, head_groups, HEAD_SIZE) * widened(attention_result).reshape(token_rows, KEY_VALUE_HEADS, head_groups, HEAD_SIZE), axis=-1))

    def block_backward_step(carry, item):
        keys_gradient_back, values_gradient_back = carry
        query_block, place_block, back_block, log_block, delta_block, index = item
        query_gradient_back, keys_gradient_back, values_gradient_back = attend_backward(query_block, place_block, back_block, log_block, delta_block, keys_rotated_pos, value_rows_local, places, index + 1, tile_piece, score_scale, keys_gradient_back, values_gradient_back)
        return ((keys_gradient_back, values_gradient_back), query_gradient_back)
    zero_filled = jnp.zeros((token_rows, KEY_VALUE_HEADS, HEAD_SIZE), jnp.float32)
    (keys_gradient_back, values_gradient_back), query_gradient_back = lax.scan(block_backward_step, (zero_filled, zero_filled), (query_block_list, position_blocks, attention_result_back.reshape(block_tally_count, tile_piece, KEY_VALUE_HEADS, head_groups, HEAD_SIZE), log_sum_blocks, delta_rows.reshape(block_tally_count, tile_piece, KEY_VALUE_HEADS, head_groups), index_list))
    query_rounded = finalize_block(apply_rotary_back(query_gradient_back.reshape(token_rows, QUERY_HEADS, HEAD_SIZE), cosine_table, sine_table).reshape(token_rows, QUERY_HEADS * HEAD_SIZE))
    key_lowered = finalize_block(apply_rotary_back(keys_gradient_back, cosine_table, sine_table).reshape(token_rows, KEY_VALUE_HEADS * HEAD_SIZE))
    value_lowered = finalize_block(values_gradient_back.reshape(token_rows, KEY_VALUE_HEADS * HEAD_SIZE))
    query_gradient = token_sum(hidden_first, query_rounded)
    key_gradient = token_sum(hidden_first, key_lowered)
    value_gradient = token_sum(hidden_first, value_lowered)
    first_back = times_transposed(query_rounded, query_matrix) + times_transposed(key_lowered, key_projection) + times_transposed(value_lowered, value_projection)
    first_gradient = lax.optimization_barrier(jnp.sum(first_back * normed_one, axis=0))
    input_back = mixed_back + norm_back(first_back, normed_one, scale_one, widened(first_scale))
    gradients = (first_gradient, query_gradient, key_gradient, value_gradient, output_gradient, second_gradient, gate_gradient, up_gradient, down_gradient)
    return (layer_output, input_back, gradients)

def reference(layer_input, positions, first_gain, query_weight, key_weight, value_proj_weight, output_weight, second_gain, gate_weight, up_weight, down_weight, cotangent):
    order = jnp.argsort(positions).astype(jnp.int32)
    inverse = jnp.argsort(order).astype(jnp.int32)
    places = jnp.take(positions, order).astype(jnp.int32)
    weights = (first_gain, query_weight, key_weight, value_proj_weight, output_weight, second_gain, gate_weight, up_weight, down_weight)
    start_offset = (jnp.zeros((MODEL_WIDTH,), jnp.float32), jnp.zeros((MODEL_WIDTH, QUERY_HEADS * HEAD_SIZE), jnp.float32), jnp.zeros((MODEL_WIDTH, KEY_VALUE_HEADS * HEAD_SIZE), jnp.float32), jnp.zeros((MODEL_WIDTH, KEY_VALUE_HEADS * HEAD_SIZE), jnp.float32), jnp.zeros((QUERY_HEADS * HEAD_SIZE, MODEL_WIDTH), jnp.float32), jnp.zeros((MODEL_WIDTH,), jnp.float32), jnp.zeros((MODEL_WIDTH, FEEDFWD_UNITS), jnp.float32), jnp.zeros((MODEL_WIDTH, FEEDFWD_UNITS), jnp.float32), jnp.zeros((FEEDFWD_UNITS, MODEL_WIDTH), jnp.float32))

    def sequence_step(totals, item):
        tokens, incoming_rows = item
        output, input_back, gradients = layer_sequence(jnp.take(tokens, order, axis=0), jnp.take(incoming_rows, order, axis=0), places, weights)
        totals = jax.tree.map(lambda left, right: left + right, totals, gradients)
        return (totals, (jnp.take(output, inverse, axis=0), jnp.take(input_back, inverse, axis=0)))
    totals, (layer_output, input_gradient) = lax.scan(sequence_step, start_offset, (layer_input, cotangent))
    return (layer_output, input_gradient, totals[0], totals[1], totals[2], totals[3], totals[4], totals[5], totals[6], totals[7], totals[8])
```

```python
import math

import jax
import jax.numpy as jnp
from jax import lax
from jax.sharding import PartitionSpec as P

QUERY_HEADS = 15
KEY_VALUE_HEADS = 5
HEAD_SIZE = 64


EPS = 1e-05
ROPE_BASE = 10000.0
NEG_FILL = -1e30
KV_SEND = jnp.bfloat16


def gather_all(piece):
    return lax.all_gather(piece, ("wsh", "ctx"), axis=0, tiled=False)


def scatter_all(pieces):
    near = lax.psum_scatter(pieces, "ctx", scatter_dimension=0, tiled=False)
    return lax.psum_scatter(near, "wsh", scatter_dimension=0, tiled=False)


def matrix_product(left, right):
    return jnp.dot(left, right, preferred_element_type=jnp.float32)


def times_transposed(left, right):
    return lax.dot_general(
        left, right, (((1,), (1,)), ((), ())), preferred_element_type=jnp.float32
    )


def token_sum(left, right):
    return lax.dot_general(
        left, right, (((0,), (0,)), ((), ())), preferred_element_type=jnp.float32
    )


def norm_scale(inputs):
    return lax.rsqrt(jnp.mean(inputs * inputs, axis=-1, keepdims=True) + EPS)


def norm_back(incoming, normed, scale, gain):
    scaled = incoming * gain
    return scale * (scaled - normed * jnp.mean(scaled * normed, axis=-1, keepdims=True))


def rope_tables(places, head_width):
    half = head_width // 2
    frequency = ROPE_BASE ** (-2.0 * jnp.arange(half, dtype=jnp.float32) / head_width)
    angle = places.astype(jnp.float32)[:, None] * frequency[None, :]
    return (jnp.cos(angle)[:, None, :], jnp.sin(angle)[:, None, :])


def apply_rotary(inputs, cosine_table, sine_table):
    half = inputs.shape[-1] // 2
    first = inputs[..., :half]
    second = inputs[..., half:]
    return jnp.concatenate(
        [first * cosine_table - second * sine_table, second * cosine_table + first * sine_table],
        axis=-1,
    )


def apply_rotary_back(incoming, cosine_table, sine_table):
    half = incoming.shape[-1] // 2
    first = incoming[..., :half]
    second = incoming[..., half:]
    return jnp.concatenate(
        [first * cosine_table + second * sine_table, second * cosine_table - first * sine_table],
        axis=-1,
    )


def attend_forward(
    query_rows_local,
    query_places,
    keys_rotated_pos,
    value_rows_local,
    key_places,
    tiles,
    tile_piece,
    score_scale,
):
    query_rows, head_groups, repeats, head_width = query_rows_local.shape

    def visit(index, carry):
        running, totals, weighted = carry
        begin = index * tile_piece
        key_tile = lax.dynamic_slice_in_dim(keys_rotated_pos, begin, tile_piece, 0)
        value_tile = lax.dynamic_slice_in_dim(value_rows_local, begin, tile_piece, 0)
        place_tile = lax.dynamic_slice_in_dim(key_places, begin, tile_piece, 0)
        scores = (
            jnp.einsum(
                "qgrd,kgd->qgrk", query_rows_local, key_tile, preferred_element_type=jnp.float32
            )
            * score_scale
        )
        allowed = (place_tile[None, :] <= query_places[:, None])[:, None, None, :]
        scores = jnp.where(allowed, scores, NEG_FILL)
        newest = jnp.maximum(running, jnp.max(scores, axis=-1))
        factor = jnp.exp(running - newest)
        portion = jnp.exp(scores - newest[..., None])
        totals = totals * factor + jnp.sum(portion, axis=-1)
        weighted = weighted * factor[..., None] + jnp.einsum(
            "qgrk,kgd->qgrd",
            portion.astype(jnp.bfloat16),
            value_tile,
            preferred_element_type=jnp.float32,
        )
        return (newest, totals, weighted)

    start_state = (
        jnp.full((query_rows, head_groups, repeats), NEG_FILL, jnp.float32),
        jnp.zeros((query_rows, head_groups, repeats), jnp.float32),
        jnp.zeros((query_rows, head_groups, repeats, head_width), jnp.float32),
    )
    running, totals, weighted = lax.fori_loop(0, tiles, visit, start_state)
    return ((weighted / totals[..., None]).astype(jnp.bfloat16), running + jnp.log(totals))


def attend_backward(
    query_rows_local,
    query_places,
    attention_result_back,
    log_total,
    delta_rows,
    keys_rotated_pos,
    value_rows_local,
    key_places,
    tiles,
    tile_piece,
    score_scale,
    keys_gradient_back,
    values_gradient_back,
):

    def visit(index, carry):
        query_gradient_back, keys_gradient_back, values_gradient_back = carry
        begin = index * tile_piece
        key_tile = lax.dynamic_slice_in_dim(keys_rotated_pos, begin, tile_piece, 0)
        value_tile = lax.dynamic_slice_in_dim(value_rows_local, begin, tile_piece, 0)
        place_tile = lax.dynamic_slice_in_dim(key_places, begin, tile_piece, 0)
        scores = (
            jnp.einsum(
                "qgrd,kgd->qgrk", query_rows_local, key_tile, preferred_element_type=jnp.float32
            )
            * score_scale
        )
        allowed = (place_tile[None, :] <= query_places[:, None])[:, None, None, :]
        scores = jnp.where(allowed, scores, NEG_FILL)
        probability = jnp.exp(scores - log_total[..., None])
        value_dots = jnp.einsum(
            "qgrd,kgd->qgrk", attention_result_back, value_tile, preferred_element_type=jnp.float32
        )
        score_grad = (probability * (value_dots - delta_rows[..., None]) * score_scale).astype(
            jnp.bfloat16
        )
        query_gradient_back = query_gradient_back + jnp.einsum(
            "qgrk,kgd->qgrd", score_grad, key_tile, preferred_element_type=jnp.float32
        )
        key_part = jnp.einsum(
            "qgrk,qgrd->kgd", score_grad, query_rows_local, preferred_element_type=jnp.float32
        )
        value_part = jnp.einsum(
            "qgrk,qgrd->kgd",
            probability.astype(jnp.bfloat16),
            attention_result_back,
            preferred_element_type=jnp.float32,
        )
        keys_gradient_back = lax.dynamic_update_slice_in_dim(
            keys_gradient_back,
            lax.dynamic_slice_in_dim(keys_gradient_back, begin, tile_piece, 0) + key_part,
            begin,
            0,
        )
        values_gradient_back = lax.dynamic_update_slice_in_dim(
            values_gradient_back,
            lax.dynamic_slice_in_dim(values_gradient_back, begin, tile_piece, 0) + value_part,
            begin,
            0,
        )
        return (query_gradient_back, keys_gradient_back, values_gradient_back)

    start_state = (
        jnp.zeros(query_rows_local.shape, jnp.float32),
        keys_gradient_back,
        values_gradient_back,
    )
    return lax.fori_loop(0, tiles, visit, start_state)


def per_device(
    layer_input,
    positions,
    first_gain,
    query_weight,
    key_weight,
    value_proj_weight,
    output_weight,
    second_gain,
    gate_weight,
    up_weight,
    down_weight,
    cotangent,
):
    parts = lax.axis_size("ctx")
    groups = lax.axis_size("wsh")
    spot = lax.axis_index("ctx")

    def spread(shard, columns):
        rows, width = shard.shape
        if columns:
            piece = lax.dynamic_slice_in_dim(shard, spot * (width // parts), width // parts, 1)
        else:
            piece = lax.dynamic_slice_in_dim(shard, spot * (rows // parts), rows // parts, 0)
        pieces = gather_all(piece)
        if columns:
            return (
                pieces.reshape(groups, parts, rows, width // parts)
                .transpose(0, 2, 1, 3)
                .reshape(groups * rows, width)
            )
        return pieces.reshape(groups * rows, width)

    gains = lax.all_gather(jnp.stack([first_gain, second_gain]), "wsh", axis=0, tiled=False)
    gains = gains.transpose(1, 0, 2).reshape(2, -1)
    first_scale, second_scale = gains[0], gains[1]
    first_matrices = spread(jnp.concatenate([query_weight, key_weight, value_proj_weight], axis=1), True)
    query_width = query_weight.shape[1]
    key_width = key_weight.shape[1]
    output_matrix = spread(output_weight, True)
    wide_matrices = spread(jnp.concatenate([gate_weight, up_weight], axis=1), True)
    down_matrix = spread(down_weight, False)
    hidden_units = gate_weight.shape[1]
    tokens = layer_input[0]
    incoming_rows = cotangent[0]
    worker_rows = tokens.shape[0]
    half_rows = worker_rows // 2
    tile_piece = 2 * worker_rows
    sequence_rows = positions.shape[0]
    head_groups = QUERY_HEADS // KEY_VALUE_HEADS
    score_scale = 1.0 / math.sqrt(HEAD_SIZE)
    own_places = lax.dynamic_slice_in_dim(
        positions, lax.axis_index("ctx") * worker_rows, worker_rows, 0
    )
    cosine_table, sine_table = rope_tables(own_places, HEAD_SIZE)
    inputs = tokens.astype(jnp.float32)
    scale_one = norm_scale(inputs)
    normed_one = inputs * scale_one
    hidden_first = (normed_one * first_scale.astype(jnp.float32)).astype(jnp.bfloat16)
    projected = matrix_product(hidden_first, first_matrices)
    query_rows_local = apply_rotary(
        projected[:, :query_width].reshape(worker_rows, QUERY_HEADS, HEAD_SIZE),
        cosine_table,
        sine_table,
    ).astype(jnp.bfloat16)
    keys_rotated_pos = apply_rotary(
        projected[:, query_width : query_width + key_width].reshape(
            worker_rows, KEY_VALUE_HEADS, HEAD_SIZE
        ),
        cosine_table,
        sine_table,
    ).astype(jnp.bfloat16)
    value_rows_local = projected[:, query_width + key_width :].astype(jnp.bfloat16)
    both = lax.all_gather(
        jnp.concatenate(
            [keys_rotated_pos.reshape(worker_rows, key_width), value_rows_local], axis=1
        ),
        "ctx",
        axis=0,
        tiled=True,
    )
    block_count = sequence_rows // half_rows
    block_ids = positions.reshape(block_count, half_rows)[:, 0] // half_rows
    slots = jnp.arange(block_count, dtype=jnp.int32)
    source = jnp.sum(jnp.where(block_ids[None, :] == slots[:, None], slots[None, :], 0), axis=1)

    def ordered_blocks(array):
        return jnp.take(
            array.reshape((block_count, half_rows) + array.shape[1:]), source, axis=0
        ).reshape(array.shape)

    def blocks_per_worker(array):
        return jnp.take(
            array.reshape((block_count, half_rows) + array.shape[1:]), block_ids, axis=0
        ).reshape(array.shape)

    both_ordered = ordered_blocks(both)
    keys_ordered = both_ordered[:, :key_width].reshape(sequence_rows, KEY_VALUE_HEADS, HEAD_SIZE)
    values_ordered = both_ordered[:, key_width:].reshape(
        sequence_rows, KEY_VALUE_HEADS, HEAD_SIZE
    )
    places_sorted = ordered_blocks(positions)
    query_head_groups = query_rows_local.reshape(
        worker_rows, KEY_VALUE_HEADS, head_groups, HEAD_SIZE
    )
    attended_parts = []
    log_parts = []
    tile_counts = []
    for half_index in range(2):
        lower = half_index * half_rows
        place_half = own_places[lower : lower + half_rows]
        needed = (jnp.max(place_half) + tile_piece) // tile_piece
        tile_counts.append(needed)
        attended_half, log_half = attend_forward(
            query_head_groups[lower : lower + half_rows],
            place_half,
            keys_ordered,
            values_ordered,
            places_sorted,
            needed,
            tile_piece,
            score_scale,
        )
        attended_parts.append(attended_half)
        log_parts.append(log_half)
    attention_result = jnp.concatenate(attended_parts, axis=0).reshape(
        worker_rows, QUERY_HEADS * HEAD_SIZE
    )
    mixed = inputs + matrix_product(attention_result, output_matrix)
    scale_two = norm_scale(mixed)
    normed_two = mixed * scale_two
    hidden_two = (normed_two * second_scale.astype(jnp.float32)).astype(jnp.bfloat16)
    wide = matrix_product(hidden_two, wide_matrices)
    gate = wide[:, :hidden_units]
    upward = wide[:, hidden_units:]
    sigma = jax.nn.sigmoid(gate)
    activated = (gate * sigma * upward).astype(jnp.bfloat16)
    layer_output = (mixed + matrix_product(activated, down_matrix)).astype(jnp.bfloat16)
    activated_back = times_transposed(incoming_rows, down_matrix)
    gate_back = (activated_back * upward * sigma * (1.0 + gate * (1.0 - sigma))).astype(
        jnp.bfloat16
    )
    up_back = (activated_back * gate * sigma).astype(jnp.bfloat16)
    wide_back = jnp.concatenate([gate_back, up_back], axis=1)
    second_back = times_transposed(wide_back, wide_matrices)
    second_gradient = jnp.sum(second_back * normed_two, axis=0)
    mixed_back = incoming_rows.astype(jnp.float32) + norm_back(
        second_back, normed_two, scale_two, second_scale.astype(jnp.float32)
    )
    mixed_low = mixed_back.astype(jnp.bfloat16)
    attention_result_back = times_transposed(mixed_low, output_matrix).astype(jnp.bfloat16)
    backward_groups = attention_result_back.reshape(
        worker_rows, KEY_VALUE_HEADS, head_groups, HEAD_SIZE
    )
    delta_rows = jnp.sum(
        backward_groups.astype(jnp.float32)
        * attention_result.reshape(worker_rows, KEY_VALUE_HEADS, head_groups, HEAD_SIZE).astype(
            jnp.float32
        ),
        axis=-1,
    )
    keys_gradient_back = jnp.zeros((sequence_rows, KEY_VALUE_HEADS, HEAD_SIZE), jnp.float32)
    values_gradient_back = jnp.zeros((sequence_rows, KEY_VALUE_HEADS, HEAD_SIZE), jnp.float32)
    query_parts = []
    for half_index in range(2):
        lower = half_index * half_rows
        query_half, keys_gradient_back, values_gradient_back = attend_backward(
            query_head_groups[lower : lower + half_rows],
            own_places[lower : lower + half_rows],
            backward_groups[lower : lower + half_rows],
            log_parts[half_index],
            delta_rows[lower : lower + half_rows],
            keys_ordered,
            values_ordered,
            places_sorted,
            tile_counts[half_index],
            tile_piece,
            score_scale,
            keys_gradient_back,
            values_gradient_back,
        )
        query_parts.append(query_half)
    query_gradient_back = jnp.concatenate(query_parts, axis=0).reshape(
        worker_rows, QUERY_HEADS, HEAD_SIZE
    )
    both_share = lax.psum_scatter(
        blocks_per_worker(
            jnp.concatenate(
                [
                    keys_gradient_back.reshape(sequence_rows, key_width),
                    values_gradient_back.reshape(sequence_rows, key_width),
                ],
                axis=1,
            ).astype(KV_SEND)
        ),
        "ctx",
        scatter_dimension=0,
        tiled=True,
    ).astype(jnp.float32)
    key_portion_local = both_share[:, :key_width]
    value_share = both_share[:, key_width:]
    query_rounded = (
        apply_rotary_back(query_gradient_back, cosine_table, sine_table)
        .reshape(worker_rows, QUERY_HEADS * HEAD_SIZE)
        .astype(jnp.bfloat16)
    )
    key_lowered = (
        apply_rotary_back(
            key_portion_local.reshape(worker_rows, KEY_VALUE_HEADS, HEAD_SIZE),
            cosine_table,
            sine_table,
        )
        .reshape(worker_rows, KEY_VALUE_HEADS * HEAD_SIZE)
        .astype(jnp.bfloat16)
    )
    value_lowered = value_share.astype(jnp.bfloat16)
    first_cols = jnp.concatenate([query_rounded, key_lowered, value_lowered], axis=1)
    first_back = times_transposed(first_cols, first_matrices)
    first_gradient = jnp.sum(first_back * normed_one, axis=0)
    input_back = mixed_back + norm_back(
        first_back, normed_one, scale_one, first_scale.astype(jnp.float32)
    )

    def collect(gradient, columns):
        rows, width = gradient.shape
        own_rows = rows // groups
        sent = gradient.astype(jnp.bfloat16)
        if columns:
            sent = sent.reshape(groups, own_rows, parts, width // parts).transpose(2, 0, 1, 3)
        else:
            sent = sent.reshape(groups, parts, own_rows // parts, width).transpose(1, 0, 2, 3)
        pieces = lax.all_gather(scatter_all(sent), "ctx", axis=0, tiled=False)
        if columns:
            pieces = pieces.transpose(1, 0, 2)
        return pieces.reshape(own_rows, width).astype(jnp.float32)

    down_total = collect(token_sum(activated, incoming_rows), False)
    wide_total = collect(token_sum(hidden_two, wide_back), True)
    output_total = collect(token_sum(attention_result, mixed_low), True)
    first_total = collect(token_sum(hidden_first, first_cols), True)
    gain_sums = lax.psum(jnp.stack([first_gradient, second_gradient]), ("wsh", "ctx"))
    own_gain = first_gain.shape[0]
    gain_sums = lax.dynamic_slice_in_dim(gain_sums, lax.axis_index("wsh") * own_gain, own_gain, 1)
    return (
        layer_output[None],
        input_back[None],
        gain_sums[0],
        first_total[:, :query_width],
        first_total[:, query_width : query_width + key_width],
        first_total[:, query_width + key_width :],
        output_total,
        gain_sums[1],
        wide_total[:, :hidden_units],
        wide_total[:, hidden_units:],
        down_total,
    )


def solution(mesh):
    in_specs = (
        P("wsh", "ctx", None),
        P(),
        P("wsh"),
        P("wsh", None),
        P("wsh", None),
        P("wsh", None),
        P("wsh", None),
        P("wsh"),
        P("wsh", None),
        P("wsh", None),
        P("wsh", None),
        P("wsh", "ctx", None),
    )
    out_specs = (
        P("wsh", "ctx", None),
        P("wsh", "ctx", None),
        P("wsh"),
        P("wsh", None),
        P("wsh", None),
        P("wsh", None),
        P("wsh", None),
        P("wsh"),
        P("wsh", None),
        P("wsh", None),
        P("wsh", None),
    )
    return jax.shard_map(
        per_device, mesh=mesh, in_specs=in_specs, out_specs=out_specs, check_vma=False
    )
```

```python
import math

import jax
import jax.numpy as jnp
from jax import lax
from jax.sharding import PartitionSpec as P

QUERY_HEADS = 15
KEY_VALUE_HEADS = 5
HEAD_SIZE = 64


EPS = 1e-05
ROPE_BASE = 10000.0
NEG_FILL = -1e30
KV_SEND = jnp.bfloat16


def gather_all(piece):
    return lax.all_gather(piece, ("wsh", "ctx"), axis=0, tiled=False)


def scatter_all(pieces):
    near = lax.psum_scatter(pieces, "ctx", scatter_dimension=0, tiled=False)
    return lax.psum_scatter(near, "wsh", scatter_dimension=0, tiled=False)


def matrix_product(left, right):
    return jnp.dot(left, right, preferred_element_type=jnp.float32)


def times_transposed(left, right):
    return lax.dot_general(
        left, right, (((1,), (1,)), ((), ())), preferred_element_type=jnp.float32
    )


def token_sum(left, right):
    return lax.dot_general(
        left, right, (((0,), (0,)), ((), ())), preferred_element_type=jnp.float32
    )


def norm_scale(inputs):
    return lax.rsqrt(jnp.mean(inputs * inputs, axis=-1, keepdims=True) + EPS)


def norm_back(incoming, normed, scale, gain):
    scaled = incoming * gain
    return scale * (scaled - normed * jnp.mean(scaled * normed, axis=-1, keepdims=True))


def rope_tables(places, head_width):
    half = head_width // 2
    frequency = ROPE_BASE ** (-2.0 * jnp.arange(half, dtype=jnp.float32) / head_width)
    angle = places.astype(jnp.float32)[:, None] * frequency[None, :]
    return (jnp.cos(angle)[:, None, :], jnp.sin(angle)[:, None, :])


def apply_rotary(inputs, cosine_table, sine_table):
    half = inputs.shape[-1] // 2
    first = inputs[..., :half]
    second = inputs[..., half:]
    return jnp.concatenate(
        [first * cosine_table - second * sine_table, second * cosine_table + first * sine_table],
        axis=-1,
    )


def apply_rotary_back(incoming, cosine_table, sine_table):
    half = incoming.shape[-1] // 2
    first = incoming[..., :half]
    second = incoming[..., half:]
    return jnp.concatenate(
        [first * cosine_table + second * sine_table, second * cosine_table - first * sine_table],
        axis=-1,
    )


def attend_forward(
    query_rows_local,
    query_places,
    keys_rotated_pos,
    value_rows_local,
    key_places,
    tiles,
    tile_piece,
    score_scale,
):
    query_rows, head_groups, repeats, head_width = query_rows_local.shape

    def visit(index, carry):
        running, totals, weighted = carry
        begin = index * tile_piece
        key_tile = lax.dynamic_slice_in_dim(keys_rotated_pos, begin, tile_piece, 0)
        value_tile = lax.dynamic_slice_in_dim(value_rows_local, begin, tile_piece, 0)
        place_tile = lax.dynamic_slice_in_dim(key_places, begin, tile_piece, 0)
        scores = (
            jnp.einsum(
                "qgrd,kgd->qgrk", query_rows_local, key_tile, preferred_element_type=jnp.float32
            )
            * score_scale
        )
        allowed = (place_tile[None, :] <= query_places[:, None])[:, None, None, :]
        scores = jnp.where(allowed, scores, NEG_FILL)
        newest = jnp.maximum(running, jnp.max(scores, axis=-1))
        factor = jnp.exp(running - newest)
        portion = jnp.exp(scores - newest[..., None])
        totals = totals * factor + jnp.sum(portion, axis=-1)
        weighted = weighted * factor[..., None] + jnp.einsum(
            "qgrk,kgd->qgrd",
            portion.astype(jnp.bfloat16),
            value_tile,
            preferred_element_type=jnp.float32,
        )
        return (newest, totals, weighted)

    start_state = (
        jnp.full((query_rows, head_groups, repeats), NEG_FILL, jnp.float32),
        jnp.zeros((query_rows, head_groups, repeats), jnp.float32),
        jnp.zeros((query_rows, head_groups, repeats, head_width), jnp.float32),
    )
    running, totals, weighted = lax.fori_loop(0, tiles, visit, start_state)
    return ((weighted / totals[..., None]).astype(jnp.bfloat16), running + jnp.log(totals))


def attend_backward(
    query_rows_local,
    query_places,
    attention_result_back,
    log_total,
    delta_rows,
    keys_rotated_pos,
    value_rows_local,
    key_places,
    tiles,
    tile_piece,
    score_scale,
    keys_gradient_back,
    values_gradient_back,
):

    def visit(index, carry):
        query_gradient_back, keys_gradient_back, values_gradient_back = carry
        begin = index * tile_piece
        key_tile = lax.dynamic_slice_in_dim(keys_rotated_pos, begin, tile_piece, 0)
        value_tile = lax.dynamic_slice_in_dim(value_rows_local, begin, tile_piece, 0)
        place_tile = lax.dynamic_slice_in_dim(key_places, begin, tile_piece, 0)
        scores = (
            jnp.einsum(
                "qgrd,kgd->qgrk", query_rows_local, key_tile, preferred_element_type=jnp.float32
            )
            * score_scale
        )
        allowed = (place_tile[None, :] <= query_places[:, None])[:, None, None, :]
        scores = jnp.where(allowed, scores, NEG_FILL)
        probability = jnp.exp(scores - log_total[..., None])
        value_dots = jnp.einsum(
            "qgrd,kgd->qgrk", attention_result_back, value_tile, preferred_element_type=jnp.float32
        )
        score_grad = (probability * (value_dots - delta_rows[..., None]) * score_scale).astype(
            jnp.bfloat16
        )
        query_gradient_back = query_gradient_back + jnp.einsum(
            "qgrk,kgd->qgrd", score_grad, key_tile, preferred_element_type=jnp.float32
        )
        key_part = jnp.einsum(
            "qgrk,qgrd->kgd", score_grad, query_rows_local, preferred_element_type=jnp.float32
        )
        value_part = jnp.einsum(
            "qgrk,qgrd->kgd",
            probability.astype(jnp.bfloat16),
            attention_result_back,
            preferred_element_type=jnp.float32,
        )
        keys_gradient_back = lax.dynamic_update_slice_in_dim(
            keys_gradient_back,
            lax.dynamic_slice_in_dim(keys_gradient_back, begin, tile_piece, 0) + key_part,
            begin,
            0,
        )
        values_gradient_back = lax.dynamic_update_slice_in_dim(
            values_gradient_back,
            lax.dynamic_slice_in_dim(values_gradient_back, begin, tile_piece, 0) + value_part,
            begin,
            0,
        )
        return (query_gradient_back, keys_gradient_back, values_gradient_back)

    start_state = (
        jnp.zeros(query_rows_local.shape, jnp.float32),
        keys_gradient_back,
        values_gradient_back,
    )
    return lax.fori_loop(0, tiles, visit, start_state)


def per_device(
    layer_input,
    positions,
    first_gain,
    query_weight,
    key_weight,
    value_proj_weight,
    output_weight,
    second_gain,
    gate_weight,
    up_weight,
    down_weight,
    cotangent,
):
    parts = lax.axis_size("ctx")
    groups = lax.axis_size("wsh")
    spot = lax.axis_index("ctx")

    def own_columns(shard):
        width = shard.shape[1] // parts
        return lax.dynamic_slice_in_dim(shard, spot * width, width, 1)

    def joined(pieces):
        rows, width = pieces.shape[1:]
        return (
            pieces.reshape(groups, parts, rows, width)
            .transpose(0, 2, 1, 3)
            .reshape(groups * rows, parts * width)
        )

    query_width = query_weight.shape[1]
    key_width = key_weight.shape[1]
    own_gain = first_gain.shape[0]
    first_piece = own_columns(
        jnp.concatenate([query_weight, key_weight, value_proj_weight], axis=1)
    )
    first_width = first_piece.shape[1]
    gain_rows = -(-2 * own_gain // first_width)

    def gain_block(pair):
        lead = pair.shape[:-1]
        pad = gain_rows * first_width - pair.shape[-1]
        filled = jnp.concatenate([pair, jnp.zeros(lead + (pad,), pair.dtype)], axis=-1)
        return filled.reshape(lead + (gain_rows, first_width))

    first_pieces = gather_all(
        jnp.concatenate(
            [first_piece, gain_block(jnp.concatenate([first_gain, second_gain]))], axis=0
        )
    )
    first_matrices = joined(first_pieces[:, :own_gain])
    gains = first_pieces.reshape(groups, parts, own_gain + gain_rows, first_width)[:, 0, own_gain:]
    gains = gains.reshape(groups, gain_rows * first_width)[:, : 2 * own_gain]
    gains = gains.reshape(groups, 2, own_gain).transpose(1, 0, 2).reshape(2, groups * own_gain)
    first_scale, second_scale = gains[0], gains[1]
    wide_piece = own_columns(jnp.concatenate([gate_weight, up_weight], axis=1))
    wide_width = wide_piece.shape[1]
    wide_pieces = gather_all(
        jnp.concatenate([wide_piece, own_columns(output_weight)], axis=1)
    )
    wide_matrices = joined(wide_pieces[..., :wide_width])
    output_matrix = joined(wide_pieces[..., wide_width:])
    down_rows = down_weight.shape[0] // parts
    down_matrix = gather_all(
        lax.dynamic_slice_in_dim(down_weight, spot * down_rows, down_rows, 0)
    ).reshape(groups * down_weight.shape[0], down_weight.shape[1])
    hidden_units = gate_weight.shape[1]
    tokens = layer_input[0]
    incoming_rows = cotangent[0]
    worker_rows = tokens.shape[0]
    half_rows = worker_rows // 2
    tile_piece = 2 * worker_rows
    sequence_rows = positions.shape[0]
    head_groups = QUERY_HEADS // KEY_VALUE_HEADS
    score_scale = 1.0 / math.sqrt(HEAD_SIZE)
    own_places = lax.dynamic_slice_in_dim(
        positions, lax.axis_index("ctx") * worker_rows, worker_rows, 0
    )
    cosine_table, sine_table = rope_tables(own_places, HEAD_SIZE)
    inputs = tokens.astype(jnp.float32)
    scale_one = norm_scale(inputs)
    normed_one = inputs * scale_one
    hidden_first = (normed_one * first_scale.astype(jnp.float32)).astype(jnp.bfloat16)
    projected = matrix_product(hidden_first, first_matrices)
    query_rows_local = apply_rotary(
        projected[:, :query_width].reshape(worker_rows, QUERY_HEADS, HEAD_SIZE),
        cosine_table,
        sine_table,
    ).astype(jnp.bfloat16)
    keys_rotated_pos = apply_rotary(
        projected[:, query_width : query_width + key_width].reshape(
            worker_rows, KEY_VALUE_HEADS, HEAD_SIZE
        ),
        cosine_table,
        sine_table,
    ).astype(jnp.bfloat16)
    value_rows_local = projected[:, query_width + key_width :].astype(jnp.bfloat16)
    both = lax.all_gather(
        jnp.concatenate(
            [keys_rotated_pos.reshape(worker_rows, key_width), value_rows_local], axis=1
        ),
        "ctx",
        axis=0,
        tiled=True,
    )
    block_count = sequence_rows // half_rows
    block_ids = positions.reshape(block_count, half_rows)[:, 0] // half_rows
    slots = jnp.arange(block_count, dtype=jnp.int32)
    source = jnp.sum(jnp.where(block_ids[None, :] == slots[:, None], slots[None, :], 0), axis=1)

    def ordered_blocks(array):
        return jnp.take(
            array.reshape((block_count, half_rows) + array.shape[1:]), source, axis=0
        ).reshape(array.shape)

    def blocks_per_worker(array):
        return jnp.take(
            array.reshape((block_count, half_rows) + array.shape[1:]), block_ids, axis=0
        ).reshape(array.shape)

    both_ordered = ordered_blocks(both)
    keys_ordered = both_ordered[:, :key_width].reshape(sequence_rows, KEY_VALUE_HEADS, HEAD_SIZE)
    values_ordered = both_ordered[:, key_width:].reshape(
        sequence_rows, KEY_VALUE_HEADS, HEAD_SIZE
    )
    places_sorted = ordered_blocks(positions)
    query_head_groups = query_rows_local.reshape(
        worker_rows, KEY_VALUE_HEADS, head_groups, HEAD_SIZE
    )
    attended_parts = []
    log_parts = []
    tile_counts = []
    for half_index in range(2):
        lower = half_index * half_rows
        place_half = own_places[lower : lower + half_rows]
        needed = (jnp.max(place_half) + tile_piece) // tile_piece
        tile_counts.append(needed)
        attended_half, log_half = attend_forward(
            query_head_groups[lower : lower + half_rows],
            place_half,
            keys_ordered,
            values_ordered,
            places_sorted,
            needed,
            tile_piece,
            score_scale,
        )
        attended_parts.append(attended_half)
        log_parts.append(log_half)
    attention_result = jnp.concatenate(attended_parts, axis=0).reshape(
        worker_rows, QUERY_HEADS * HEAD_SIZE
    )
    mixed = inputs + matrix_product(attention_result, output_matrix)
    scale_two = norm_scale(mixed)
    normed_two = mixed * scale_two
    hidden_two = (normed_two * second_scale.astype(jnp.float32)).astype(jnp.bfloat16)
    wide = matrix_product(hidden_two, wide_matrices)
    gate = wide[:, :hidden_units]
    upward = wide[:, hidden_units:]
    sigma = jax.nn.sigmoid(gate)
    activated = (gate * sigma * upward).astype(jnp.bfloat16)
    layer_output = (mixed + matrix_product(activated, down_matrix)).astype(jnp.bfloat16)
    activated_back = times_transposed(incoming_rows, down_matrix)
    gate_back = (activated_back * upward * sigma * (1.0 + gate * (1.0 - sigma))).astype(
        jnp.bfloat16
    )
    up_back = (activated_back * gate * sigma).astype(jnp.bfloat16)
    wide_back = jnp.concatenate([gate_back, up_back], axis=1)
    second_back = times_transposed(wide_back, wide_matrices)
    second_gradient = jnp.sum(second_back * normed_two, axis=0)
    mixed_back = incoming_rows.astype(jnp.float32) + norm_back(
        second_back, normed_two, scale_two, second_scale.astype(jnp.float32)
    )
    mixed_low = mixed_back.astype(jnp.bfloat16)
    attention_result_back = times_transposed(mixed_low, output_matrix).astype(jnp.bfloat16)

    def cut(gradient):
        rows, width = gradient.shape
        return (
            gradient.astype(jnp.bfloat16)
            .reshape(groups, rows // groups, parts, width // parts)
            .transpose(2, 0, 1, 3)
        )

    splits = own_gain // down_rows
    down_width = down_weight.shape[1] // splits
    down_blocks = [
        token_sum(activated, incoming_rows[:, index * down_width : (index + 1) * down_width])
        .astype(jnp.bfloat16)
        .reshape(groups, parts, down_rows, down_width)
        .transpose(1, 0, 2, 3)
        for index in range(splits)
    ]
    wide_sent = jnp.concatenate(
        [
            cut(token_sum(hidden_two, wide_back)),
            jnp.concatenate(down_blocks, axis=2),
            cut(token_sum(attention_result, mixed_low)),
        ],
        axis=-1,
    )
    wide_sent, attention_result_back = lax.optimization_barrier(
        (wide_sent, attention_result_back)
    )
    wide_near = lax.psum_scatter(wide_sent, "ctx", scatter_dimension=0, tiled=False)
    backward_groups = attention_result_back.reshape(
        worker_rows, KEY_VALUE_HEADS, head_groups, HEAD_SIZE
    )
    delta_rows = jnp.sum(
        backward_groups.astype(jnp.float32)
        * attention_result.reshape(worker_rows, KEY_VALUE_HEADS, head_groups, HEAD_SIZE).astype(
            jnp.float32
        ),
        axis=-1,
    )
    keys_gradient_back = jnp.zeros((sequence_rows, KEY_VALUE_HEADS, HEAD_SIZE), jnp.float32)
    values_gradient_back = jnp.zeros((sequence_rows, KEY_VALUE_HEADS, HEAD_SIZE), jnp.float32)
    query_parts = []
    for half_index in range(2):
        lower = half_index * half_rows
        query_half, keys_gradient_back, values_gradient_back = attend_backward(
            query_head_groups[lower : lower + half_rows],
            own_places[lower : lower + half_rows],
            backward_groups[lower : lower + half_rows],
            log_parts[half_index],
            delta_rows[lower : lower + half_rows],
            keys_ordered,
            values_ordered,
            places_sorted,
            tile_counts[half_index],
            tile_piece,
            score_scale,
            keys_gradient_back,
            values_gradient_back,
        )
        query_parts.append(query_half)
    query_gradient_back = jnp.concatenate(query_parts, axis=0).reshape(
        worker_rows, QUERY_HEADS, HEAD_SIZE
    )
    wide_near, keys_gradient_back, values_gradient_back = lax.optimization_barrier(
        (wide_near, keys_gradient_back, values_gradient_back)
    )
    both_share = lax.psum_scatter(
        blocks_per_worker(
            jnp.concatenate(
                [
                    keys_gradient_back.reshape(sequence_rows, key_width),
                    values_gradient_back.reshape(sequence_rows, key_width),
                ],
                axis=1,
            ).astype(KV_SEND)
        ),
        "ctx",
        scatter_dimension=0,
        tiled=True,
    ).astype(jnp.float32)
    key_portion_local = both_share[:, :key_width]
    value_share = both_share[:, key_width:]
    query_rounded = (
        apply_rotary_back(query_gradient_back, cosine_table, sine_table)
        .reshape(worker_rows, QUERY_HEADS * HEAD_SIZE)
        .astype(jnp.bfloat16)
    )
    key_lowered = (
        apply_rotary_back(
            key_portion_local.reshape(worker_rows, KEY_VALUE_HEADS, HEAD_SIZE),
            cosine_table,
            sine_table,
        )
        .reshape(worker_rows, KEY_VALUE_HEADS * HEAD_SIZE)
        .astype(jnp.bfloat16)
    )
    value_lowered = value_share.astype(jnp.bfloat16)
    first_cols = jnp.concatenate([query_rounded, key_lowered, value_lowered], axis=1)
    first_back = times_transposed(first_cols, first_matrices)
    first_gradient = jnp.sum(first_back * normed_one, axis=0)
    input_back = mixed_back + norm_back(
        first_back, normed_one, scale_one, first_scale.astype(jnp.float32)
    )

    def own_rows_of(pieces):
        count, rows, width = pieces.shape
        return pieces.transpose(1, 0, 2).reshape(rows, count * width).astype(jnp.float32)

    wide_share = lax.psum_scatter(wide_near, "wsh", scatter_dimension=0, tiled=False)
    wide_total = lax.all_gather(wide_share, "ctx", axis=0, tiled=False)
    output_total = own_rows_of(wide_total[..., wide_width + down_width :])
    down_total = (
        wide_total[..., wide_width : wide_width + down_width]
        .reshape(parts, splits, down_rows, down_width)
        .transpose(0, 2, 1, 3)
        .reshape(down_weight.shape)
        .astype(jnp.float32)
    )
    wide_total = own_rows_of(wide_total[..., :wide_width])
    gain_pair = jnp.stack([first_gradient, second_gradient]).astype(jnp.bfloat16)
    gain_pair = gain_pair.reshape(2, groups, own_gain).transpose(1, 0, 2)
    gain_pair = gain_block(gain_pair.reshape(groups, 2 * own_gain))
    first_sent = jnp.concatenate(
        [
            cut(token_sum(hidden_first, first_cols)),
            jnp.broadcast_to(gain_pair[None], (parts,) + gain_pair.shape),
        ],
        axis=2,
    )
    first_total = lax.all_gather(scatter_all(first_sent), "ctx", axis=0, tiled=False)
    gain_sums = first_total[0, own_gain:].reshape(gain_rows * first_width)[: 2 * own_gain]
    gain_sums = gain_sums.reshape(2, own_gain).astype(jnp.float32)
    first_total = own_rows_of(first_total[:, :own_gain])
    return (
        layer_output[None],
        input_back[None],
        gain_sums[0],
        first_total[:, :query_width],
        first_total[:, query_width : query_width + key_width],
        first_total[:, query_width + key_width :],
        output_total,
        gain_sums[1],
        wide_total[:, :hidden_units],
        wide_total[:, hidden_units:],
        down_total,
    )


def solution(mesh):
    in_specs = (
        P("wsh", "ctx", None),
        P(),
        P("wsh"),
        P("wsh", None),
        P("wsh", None),
        P("wsh", None),
        P("wsh", None),
        P("wsh"),
        P("wsh", None),
        P("wsh", None),
        P("wsh", None),
        P("wsh", "ctx", None),
    )
    out_specs = (
        P("wsh", "ctx", None),
        P("wsh", "ctx", None),
        P("wsh"),
        P("wsh", None),
        P("wsh", None),
        P("wsh", None),
        P("wsh", None),
        P("wsh"),
        P("wsh", None),
        P("wsh", None),
        P("wsh", None),
    )
    return jax.shard_map(
        per_device, mesh=mesh, in_specs=in_specs, out_specs=out_specs, check_vma=False
    )
```
